256 devices in a mesh: gx: 16 (over y, x_lo, core), gy: 16 (over x_hi, z).
Axes of the slice: x: 4 (x_hi: 2, x_lo: 2; x = x_hi * 2 + x_lo), y: 4, z: 8, core: 2. Of those that a mesh axis runs over, the one named last changes fastest.
Arguments:
- blocks: bfloat16 [16, 16, 128, 128, 128], P('gx', 'gy'), may hold values from -0.1875 to 0.1875
- pattern: int32 [16, 16, 128], P('gx', 'gy'), may hold values from 0 to 255, as said below
- local_src: bfloat16 [16, 16, 2, 32, 2048], P('gx', 'gy'), may hold values from -4 to 4
- owner: int32 [2, 32], replicated, may hold values from 0 to 255
Outputs:
- sweep_out: bfloat16 [16, 16, 2, 32, 2048], P('gx', 'gy')
The draws below stay inside these ranges and needn't reach their ends.
Inputs may be any that keep to these rules, and one draw needn't show every extreme that they name: `pattern`: the 128 values of one cell are distinct.
All inputs are finite; a program needn't handle non-finite values.
Results may differ from the reference program's by a relative error of at most 0.019.
Values may be sent and summed in bfloat16 or wider, within the bound.
No kernel may reach another device: no remote copies, remote signals or barrier semaphores. Data moves between devices by JAX's collectives and lax.ppermute only.
A program may use at most 64 MiB of HBM per device.

```python
import jax
import jax.numpy as jnp
from jax import lax

TR = 1024
BS = 128
NBLK = 16
NNZ = 128
S = 32
NB = 2
NX = 16
NY = 16


def draw_pattern(key, part):
    keys = jax.random.split(key, NX * NY)
    perms = jax.vmap(lambda one_key: jax.random.permutation(one_key, NBLK * NBLK))(keys)
    return perms[:, :NNZ].reshape(NX, NY, NNZ).astype(jnp.int32)


def set_ends(values, stream_key, smallest, high):
    longest = values.shape.index(max(values.shape))
    spots = []
    for shift in (0, 1):
        where = [jax.random.randint(jax.random.fold_in(stream_key, axis), (), 0, length) for axis, length in enumerate(values.shape)]
        where[longest] = (where[longest] + shift) % values.shape[longest]
        spots.append(tuple(where))
    return values.at[spots[0]].set(smallest).at[spots[1]].set(high)


def block_scale(own_key, dims, cuts, low, high):
    factor_of = 1.0
    for dim, parts in cuts:
        steps = jax.random.uniform(jax.random.fold_in(jax.random.fold_in(own_key, 6), dim), (parts,), jnp.float32, low / len(cuts), high / len(cuts))
        factor_of = factor_of * jnp.repeat(jnp.exp(steps), dims[dim] // parts).reshape((-1,) + (1,) * (len(dims) - 1 - dim))
    return factor_of


def centred(rng, dims, spread, limit, pieces=(), kind=jnp.bfloat16):
    gain = block_scale(rng, dims, pieces, -0.22, 0.18) if pieces else 1.0
    drawn = jax.random.normal(rng, dims, jnp.float32) * spread * gain
    return jnp.minimum(jnp.maximum(drawn, -limit), limit).astype(kind)


def setup_inputs(seed: int = 0) -> dict:
    key_of = jax.random.split(jax.random.key(seed), 5)
    return {
        "blocks": centred(key_of[0], (NX, NY, NNZ, BS, BS), (NNZ * BS * BS // (2 * TR)) ** -0.5, 0.1875, ((0, 16), (1, 16))),
        "pattern": draw_pattern(jax.random.fold_in(key_of[4], 71), 0),
        "local_src": centred(key_of[2], (NX, NY, NB, S, 2 * TR), 0.5, 4.0, ((0, 16), (1, 16))),
        "owner": set_ends(jax.random.randint(key_of[3], (NB, S), 0, NX * NY), jax.random.fold_in(key_of[3], 1), 0, (NX * NY) - 1).astype(jnp.int32),
    }


def cell_matrix(blk, pat):
    dense = jnp.zeros((NBLK * NBLK, BS, BS), blk.dtype).at[pat].set(blk)
    return dense.reshape(NBLK, NBLK, BS, BS).transpose(0, 2, 1, 3).reshape(2 * TR, 2 * TR)


def reference(blocks, pattern, local_src, owner):
    cell_ids = jnp.arange(NX * NY, dtype=jnp.int32).reshape(NX, NY)

    def column(left_all, column_data):
        blk_col, pat_col, src_col, id_col = column_data

        def cell(bottom, cell_data):
            left, blk, pat, src, cell_id = cell_data
            joined = jnp.concatenate([left, bottom], axis=2).reshape(NB * S, 2 * TR)
            matrix = cell_matrix(blk, pat)
            total = jnp.dot(joined, matrix.T, preferred_element_type=jnp.float32).reshape(NB, S, 2 * TR)
            mask = (owner == cell_id).astype(jnp.float32)
            total = total + src.astype(jnp.float32) * mask[:, :, None]
            result = total.astype(jnp.bfloat16)
            return result[:, :, TR:], result

        zero = jnp.zeros((NB, S, TR), jnp.bfloat16)
        _, results = lax.scan(cell, zero, (left_all, blk_col, pat_col, src_col, id_col))
        return results[:, :, :, :TR], results

    start = jnp.zeros((NY, NB, S, TR), jnp.bfloat16)
    _, outputs = lax.scan(column, start, (blocks, pattern, local_src, cell_ids))
    return outputs
```

```python
import jax
import jax.numpy as jnp
from jax import lax
from jax.experimental import pallas as pl
from jax.experimental.pallas import tpu as pltpu
from jax.sharding import PartitionSpec as P

VMEM = pl.BlockSpec(memory_space=pltpu.VMEM)
SMEM = pl.BlockSpec(memory_space=pltpu.SMEM)
PARAMS = pltpu.CompilerParams(vmem_limit_bytes=16 * 2**20)


def assemble_kernel(pat, blk, dense):
    count, order, _ = blk.shape
    nblk = dense.shape[0] // order
    dense[...] = jnp.zeros_like(dense)

    def place(k, _):
        row = pl.multiple_of(pat[k] // nblk * order, order)
        col = pl.multiple_of(pat[k] % nblk * order, order)
        dense[pl.ds(col, order), pl.ds(row, order)] = blk[k].T
        return 0

    lax.fori_loop(0, count, place, 0, unroll=8)


def assemble(pat, blk, width):
    return pl.pallas_call(
        assemble_kernel,
        out_shape=pltpu.VMEM((width, width), blk.dtype),
        in_specs=[SMEM, VMEM],
        out_specs=VMEM,
        compiler_params=PARAMS,
        name="assemble",
    )(pat, blk)


def first_kernel(turn, position, dense, source, left, _, total):
    @pl.when(position[0] == turn)
    def _():
        part = jnp.dot(left[...], dense[: left.shape[1]], preferred_element_type=jnp.float32)
        total[...] = part + source[...].astype(jnp.float32)


def second_kernel(turn, half, position, dense, total, bottom, _, out):
    @pl.when(position[0] == turn)
    def _():
        trace = bottom.shape[1]
        cols = slice(half * trace, (half + 1) * trace)
        part = jnp.dot(bottom[...], dense[trace:, cols], preferred_element_type=jnp.float32)
        out[...] = (total[:, cols] + part).astype(out.dtype)


def first(turn, position, dense, source, left, total):
    return pl.pallas_call(
        lambda *refs: first_kernel(turn, *refs),
        out_shape=jax.ShapeDtypeStruct(total.shape, total.dtype),
        in_specs=[SMEM] + [VMEM] * 4,
        out_specs=VMEM,
        input_output_aliases={4: 0},
        compiler_params=PARAMS,
        name="first",
    )(position, dense, source, left, total)


def second(turn, half, position, dense, total, bottom, out):
    return pl.pallas_call(
        lambda *refs: second_kernel(turn, half, *refs),
        out_shape=jax.ShapeDtypeStruct(out.shape, out.dtype),
        in_specs=[SMEM] + [VMEM] * 4,
        out_specs=VMEM,
        input_output_aliases={4: 0},
        compiler_params=PARAMS,
        name="right" if half == 0 else "top",
    )(position, dense, total, bottom, out)


def pairs(nx, ny, turn, period, across):
    found = []
    for i in range(nx):
        for j in range(ny):
            over, up = (i + 1, j) if across else (i, j + 1)
            if (i + j) % period == turn % period and over < nx and up < ny:
                found.append((i * ny + j, over * ny + up))
    return found


def body(blocks, pattern, local_src, owner):
    nbatch, nsource, width = local_src.shape[2:]
    rows = nbatch * nsource
    trace = width // 2
    period = 16
    nx, ny = lax.axis_size("gx"), lax.axis_size("gy")
    dense = assemble(pattern[0, 0], blocks[0, 0], width)
    x, y = lax.axis_index("gx"), lax.axis_index("gy")
    mine = (owner == x * ny + y).reshape(rows, 1)
    own = local_src[0, 0].reshape(rows, width)
    source = jnp.where(mine, own, jnp.zeros_like(own))
    position = (x + y).reshape(1)
    left = bottom = right = top = jnp.zeros((rows, trace), local_src.dtype)
    total = jnp.zeros((rows, width), jnp.float32)
    last = nx + ny - 2
    for turn in range(last + 1):
        total = first(turn, position, dense, source, left, total)
        right = second(turn, 0, position, dense, total, bottom, right)
        top = second(turn, 1, position, dense, total, bottom, top)
        if turn < last:
            left = lax.ppermute(right, ("gx", "gy"), pairs(nx, ny, turn, period, True))
            bottom = lax.ppermute(top, ("gx", "gy"), pairs(nx, ny, turn, period, False))
    result = jnp.concatenate([right, top], axis=1)
    return result.reshape(1, 1, nbatch, nsource, width)


def solution(mesh):
    return jax.shard_map(
        body,
        mesh=mesh,
        in_specs=(
            P("gx", "gy", None, None, None),
            P("gx", "gy", None),
            P("gx", "gy", None, None, None),
            P(),
        ),
        out_specs=P("gx", "gy", None, None, None),
        check_vma=False,
    )
```

```python
import jax
import jax.numpy as jnp
from jax import lax
from jax.experimental import pallas as pl
from jax.experimental.pallas import tpu as pltpu
from jax.sharding import PartitionSpec as P

VMEM = pl.BlockSpec(memory_space=pltpu.VMEM)
SMEM = pl.BlockSpec(memory_space=pltpu.SMEM)
PARAMS = pltpu.CompilerParams(vmem_limit_bytes=4 * 2**20)


def assemble_kernel(pat, blk, dense):
    count, order, _ = blk.shape
    nblk = dense.shape[0] // order
    dense[...] = jnp.zeros_like(dense)

    def place(k, _):
        row = pl.multiple_of(pat[k] // nblk * order, order)
        col = pl.multiple_of(pat[k] % nblk * order, order)
        dense[pl.ds(col, order), pl.ds(row, order)] = blk[k].T
        return 0

    lax.fori_loop(0, count, place, 0, unroll=8)


def assemble(pat, blk, width):
    return pl.pallas_call(
        assemble_kernel,
        out_shape=pltpu.VMEM((width, width), blk.dtype),
        in_specs=[SMEM, VMEM],
        out_specs=VMEM,
        compiler_params=PARAMS,
        name="assemble",
    )(pat, blk)


def first_kernel(turn, position, dense, source, left, total):
    @pl.when(position[0] == turn)
    def _():
        def columns(n, _):
            cols = pl.ds(pl.multiple_of(n * chunk, chunk), chunk)
            part = jnp.dot(left[...], dense[:trace, cols], preferred_element_type=jnp.float32)
            total[:, cols] = part + source[:, cols].astype(jnp.float32)
            return 0

        trace = left.shape[1]
        chunk = trace // 1
        lax.fori_loop(0, total.shape[1] // chunk, columns, 0)


def second_kernel(turn, half, position, dense, total, bottom, _, out):
    @pl.when(position[0] == turn)
    def _():
        trace = bottom.shape[1]
        cols = slice(half * trace, (half + 1) * trace)
        part = jnp.dot(bottom[...], dense[trace:, cols], preferred_element_type=jnp.float32)
        out[...] = (total[:, cols] + part).astype(out.dtype)


def first(turn, position, dense, source, left):
    return pl.pallas_call(
        lambda *refs: first_kernel(turn, *refs),
        out_shape=pltpu.VMEM(source.shape, jnp.float32),
        in_specs=[SMEM] + [VMEM] * 3,
        out_specs=VMEM,
        compiler_params=PARAMS,
        name="first",
    )(position, dense, source, left)


def second(turn, half, position, dense, total, bottom, out):
    return pl.pallas_call(
        lambda *refs: second_kernel(turn, half, *refs),
        out_shape=jax.ShapeDtypeStruct(out.shape, out.dtype),
        in_specs=[SMEM] + [VMEM] * 4,
        out_specs=VMEM,
        input_output_aliases={4: 0},
        compiler_params=PARAMS,
        name="right" if half == 0 else "top",
    )(position, dense, total, bottom, out)


def pairs(nx, ny, turn, period, across):
    found = []
    for i in range(nx):
        for j in range(ny):
            over, up = (i + 1, j) if across else (i, j + 1)
            if (i + j) % period == turn % period and over < nx and up < ny:
                found.append((i * ny + j, over * ny + up))
    return found


def body(blocks, pattern, local_src, owner):
    nbatch, nsource, width = local_src.shape[2:]
    rows = nbatch * nsource
    trace = width // 2
    period = 16
    nx, ny = lax.axis_size("gx"), lax.axis_size("gy")
    dense = assemble(pattern[0, 0], blocks[0, 0], width)
    x, y = lax.axis_index("gx"), lax.axis_index("gy")
    mine = (owner == x * ny + y)[:, :, None]
    own = local_src[0, 0]
    source = jnp.where(mine, own, jnp.zeros_like(own)).reshape(rows, width)
    position = (x + y).reshape(1)

    right, top = source[:, :trace], source[:, trace:]
    for turn in range(1, nx + ny - 1):
        left = lax.ppermute(right, ("gx", "gy"), pairs(nx, ny, turn - 1, period, True))
        bottom = lax.ppermute(top, ("gx", "gy"), pairs(nx, ny, turn - 1, period, False))
        total = first(turn, position, dense, source, left)
        right = second(turn, 0, position, dense, total, bottom, right)
        top = second(turn, 1, position, dense, total, bottom, top)
    result = jnp.concatenate([right, top], axis=1)
    return result.reshape(1, 1, nbatch, nsource, width)


def solution(mesh):
    return jax.shard_map(
        body,
        mesh=mesh,
        in_specs=(
            P("gx", "gy", None, None, None),
            P("gx", "gy", None),
            P("gx", "gy", None, None, None),
            P(),
        ),
        out_specs=P("gx", "gy", None, None, None),
        check_vma=False,
    )
```

```python
import jax
import jax.numpy as jnp
from jax import lax
from jax.experimental import pallas as pl
from jax.experimental.pallas import tpu as pltpu
from jax.sharding import PartitionSpec as P

VMEM = pl.BlockSpec(memory_space=pltpu.VMEM)
SMEM = pl.BlockSpec(memory_space=pltpu.SMEM)
HBM = pl.BlockSpec(memory_space=pltpu.HBM)
PIECES = 8
PARAMS = pltpu.CompilerParams(vmem_limit_bytes=4 * 2**20)


def assemble_kernel(pattern, blocks, dense, pat, blk, pat_done, blk_done):
    count, order, _ = blk.shape
    nblk = dense.shape[0] // order
    pieces = blk_done.shape[0]
    piece = count // pieces
    pat_copy = pltpu.make_async_copy(pattern, pat, pat_done)
    pat_copy.start()

    def blk_copy(p):
        part = pl.ds(p * piece, piece)
        return pltpu.make_async_copy(blocks.at[part], blk.at[part], blk_done.at[p])

    for p in range(pieces):
        blk_copy(p).start()
    dense[...] = jnp.zeros_like(dense)
    pat_copy.wait()

    def settle(p, _):
        blk_copy(p).wait()

        def place(n, _):
            k = p * piece + n
            row = pl.multiple_of(pat[k] // nblk * order, order)
            col = pl.multiple_of(pat[k] % nblk * order, order)
            dense[pl.ds(col, order), pl.ds(row, order)] = blk[k].T
            return 0

        lax.fori_loop(0, piece, place, 0, unroll=8)
        return 0

    lax.fori_loop(0, pieces, settle, 0)


def assemble(pat, blk, width):
    return pl.pallas_call(
        assemble_kernel,
        out_shape=pltpu.VMEM((width, width), blk.dtype),
        in_specs=[HBM, HBM],
        out_specs=VMEM,
        scratch_shapes=[
            pltpu.SMEM(pat.shape, pat.dtype),
            pltpu.VMEM(blk.shape, blk.dtype),
            pltpu.SemaphoreType.DMA,
            pltpu.SemaphoreType.DMA((PIECES,)),
        ],
        compiler_params=pltpu.CompilerParams(vmem_limit_bytes=8 * 2**20),
        name="assemble",
    )(pltpu.with_memory_space_constraint(pat, pltpu.HBM), pltpu.with_memory_space_constraint(blk, pltpu.HBM))


def source_kernel(cell, owner, local, source, right, top, held, who, local_done, who_done):
    local_copy = pltpu.make_async_copy(local, held, local_done)
    who_copy = pltpu.make_async_copy(owner, who, who_done)
    who_copy.start()
    local_copy.start()
    nbatch, nsource, width = held.shape
    trace = width // 2
    square = (nsource, nsource)
    diagonal = lax.broadcasted_iota(jnp.int32, square, 0) == lax.broadcasted_iota(jnp.int32, square, 1)
    who_copy.wait()
    mine = []
    for b in range(nbatch):
        row = jnp.broadcast_to((who[b : b + 1, :] == cell[0]).astype(jnp.float32), square)
        mine.append(jnp.max(jnp.where(diagonal, row, 0.0), axis=1, keepdims=True) > 0.0)
    local_copy.wait()
    for b in range(nbatch):
        rows = slice(b * nsource, (b + 1) * nsource)
        own = jnp.where(mine[b], held[b].astype(jnp.float32), 0.0).astype(source.dtype)
        source[rows, :] = own
        right[rows, :] = own[:, :trace]
        top[rows, :] = own[:, trace:]


def sources(cell, owner, local):
    nbatch, nsource, width = local.shape
    rows = nbatch * nsource
    half = jax.ShapeDtypeStruct((rows, width // 2), local.dtype)
    return pl.pallas_call(
        source_kernel,
        out_shape=(jax.ShapeDtypeStruct((rows, width), local.dtype), half, half),
        in_specs=[SMEM, HBM, HBM],
        out_specs=(VMEM, VMEM, VMEM),
        scratch_shapes=[
            pltpu.VMEM(local.shape, local.dtype),
            pltpu.VMEM(owner.shape, owner.dtype),
            pltpu.SemaphoreType.DMA,
            pltpu.SemaphoreType.DMA,
        ],
        compiler_params=PARAMS,
        name="sources",
    )(cell, pltpu.with_memory_space_constraint(owner, pltpu.HBM), pltpu.with_memory_space_constraint(local, pltpu.HBM))


def first_kernel(turn, position, dense, source, left, total):
    @pl.when(position[0] == turn)
    def _():
        def columns(n, _):
            cols = pl.ds(pl.multiple_of(n * chunk, chunk), chunk)
            part = jnp.dot(left[...], dense[:trace, cols], preferred_element_type=jnp.float32)
            total[:, cols] = part + source[:, cols].astype(jnp.float32)
            return 0

        trace = left.shape[1]
        chunk = trace // 1
        lax.fori_loop(0, total.shape[1] // chunk, columns, 0)


def second_kernel(turn, half, position, dense, total, bottom, _, out):
    @pl.when(position[0] == turn)
    def _():
        trace = bottom.shape[1]
        cols = slice(half * trace, (half + 1) * trace)
        part = jnp.dot(bottom[...], dense[trace:, cols], preferred_element_type=jnp.float32)
        out[...] = (total[:, cols] + part).astype(out.dtype)


def first(turn, position, dense, source, left):
    return pl.pallas_call(
        lambda *refs: first_kernel(turn, *refs),
        out_shape=pltpu.VMEM(source.shape, jnp.float32),
        in_specs=[SMEM] + [VMEM] * 3,
        out_specs=VMEM,
        compiler_params=PARAMS,
        name="first",
    )(position, dense, source, left)


def second(turn, half, position, dense, total, bottom, out):
    return pl.pallas_call(
        lambda *refs: second_kernel(turn, half, *refs),
        out_shape=jax.ShapeDtypeStruct(out.shape, out.dtype),
        in_specs=[SMEM] + [VMEM] * 4,
        out_specs=VMEM,
        input_output_aliases={4: 0},
        compiler_params=PARAMS,
        name="right" if half == 0 else "top",
    )(position, dense, total, bottom, out)


def pairs(nx, ny, turn, period, across):
    found = []
    for i in range(nx):
        for j in range(ny):
            over, up = (i + 1, j) if across else (i, j + 1)
            if (i + j) % period == turn % period and over < nx and up < ny:
                found.append((i * ny + j, over * ny + up))
    return found


def body(blocks, pattern, local_src, owner):
    nbatch, nsource, width = local_src.shape[2:]
    trace = width // 2
    period = 16
    nx, ny = lax.axis_size("gx"), lax.axis_size("gy")
    dense = assemble(pattern[0, 0], blocks[0, 0], width)
    x, y = lax.axis_index("gx"), lax.axis_index("gy")
    source, right, top = sources((x * ny + y).reshape(1), owner, local_src[0, 0])
    position = (x + y).reshape(1)

    for turn in range(1, nx + ny - 1):
        left = lax.ppermute(right, ("gx", "gy"), pairs(nx, ny, turn - 1, period, True))
        bottom = lax.ppermute(top, ("gx", "gy"), pairs(nx, ny, turn - 1, period, False))
        total = first(turn, position, dense, source, left)
        right = second(turn, 0, position, dense, total, bottom, right)
        top = second(turn, 1, position, dense, total, bottom, top)
    result = jnp.concatenate([right, top], axis=1)
    return result.reshape(1, 1, nbatch, nsource, width)


def solution(mesh):
    return jax.shard_map(
        body,
        mesh=mesh,
        in_specs=(
            P("gx", "gy", None, None, None),
            P("gx", "gy", None),
            P("gx", "gy", None, None, None),
            P(),
        ),
        out_specs=P("gx", "gy", None, None, None),
        check_vma=False,
    )
```

```python
import jax
import jax.numpy as jnp
from jax import lax
from jax.experimental import pallas as pl
from jax.experimental.pallas import tpu as pltpu
from jax.sharding import PartitionSpec as P

VMEM = pl.BlockSpec(memory_space=pltpu.VMEM)
SMEM = pl.BlockSpec(memory_space=pltpu.SMEM)
HBM = pl.BlockSpec(memory_space=pltpu.HBM)
PIECES = 8
PARAMS = pltpu.CompilerParams(vmem_limit_bytes=4 * 2**20)


def assemble_kernel(pattern, blocks, dense, pat, blk, pat_done, blk_done):
    count, order, _ = blk.shape
    nblk = dense.shape[0] // order
    pieces = blk_done.shape[0]
    piece = count // pieces
    pat_copy = pltpu.make_async_copy(pattern, pat, pat_done)
    pat_copy.start()

    def blk_copy(p):
        part = pl.ds(p * piece, piece)
        return pltpu.make_async_copy(blocks.at[part], blk.at[part], blk_done.at[p])

    for p in range(pieces):
        blk_copy(p).start()
    dense[...] = jnp.zeros_like(dense)
    pat_copy.wait()

    def settle(p, _):
        blk_copy(p).wait()

        def place(n, _):
            k = p * piece + n
            row = pl.multiple_of(pat[k] // nblk * order, order)
            col = pl.multiple_of(pat[k] % nblk * order, order)
            dense[pl.ds(col, order), pl.ds(row, order)] = blk[k].T
            return 0

        lax.fori_loop(0, piece, place, 0, unroll=8)
        return 0

    lax.fori_loop(0, pieces, settle, 0)


def assemble(pat, blk, width):
    return pl.pallas_call(
        assemble_kernel,
        out_shape=pltpu.VMEM((width, width), blk.dtype),
        in_specs=[HBM, HBM],
        out_specs=VMEM,
        scratch_shapes=[
            pltpu.SMEM(pat.shape, pat.dtype),
            pltpu.VMEM(blk.shape, blk.dtype),
            pltpu.SemaphoreType.DMA,
            pltpu.SemaphoreType.DMA((PIECES,)),
        ],
        compiler_params=pltpu.CompilerParams(vmem_limit_bytes=8 * 2**20),
        name="assemble",
    )(pltpu.with_memory_space_constraint(pat, pltpu.HBM), pltpu.with_memory_space_constraint(blk, pltpu.HBM))


def source_kernel(cell, owner, local, source, right, top, held, who, local_done, who_done):
    local_copy = pltpu.make_async_copy(local, held, local_done)
    who_copy = pltpu.make_async_copy(owner, who, who_done)
    who_copy.start()
    local_copy.start()
    nbatch, nsource, width = held.shape
    trace = width // 2
    square = (nsource, nsource)
    diagonal = lax.broadcasted_iota(jnp.int32, square, 0) == lax.broadcasted_iota(jnp.int32, square, 1)
    who_copy.wait()
    mine = []
    for b in range(nbatch):
        row = jnp.broadcast_to((who[b : b + 1, :] == cell[0]).astype(jnp.float32), square)
        mine.append(jnp.max(jnp.where(diagonal, row, 0.0), axis=1, keepdims=True) > 0.0)
    local_copy.wait()
    for b in range(nbatch):
        rows = slice(b * nsource, (b + 1) * nsource)
        own = jnp.where(mine[b], held[b].astype(jnp.float32), 0.0).astype(source.dtype)
        source[rows, :] = own
        right[rows, :] = own[:, :trace]
        top[rows, :] = own[:, trace:]


def sources(cell, owner, local):
    nbatch, nsource, width = local.shape
    rows = nbatch * nsource
    half = jax.ShapeDtypeStruct((rows, width // 2), local.dtype)
    return pl.pallas_call(
        source_kernel,
        out_shape=(jax.ShapeDtypeStruct((rows, width), local.dtype), half, half),
        in_specs=[SMEM, HBM, HBM],
        out_specs=(VMEM, VMEM, VMEM),
        scratch_shapes=[
            pltpu.VMEM(local.shape, local.dtype),
            pltpu.VMEM(owner.shape, owner.dtype),
            pltpu.SemaphoreType.DMA,
            pltpu.SemaphoreType.DMA,
        ],
        compiler_params=PARAMS,
        name="sources",
    )(cell, pltpu.with_memory_space_constraint(owner, pltpu.HBM), pltpu.with_memory_space_constraint(local, pltpu.HBM))


def first_kernel(turn, position, dense, source, bottom, total):
    @pl.when(position[0] == turn)
    def _():
        def columns(n, _):
            cols = pl.ds(pl.multiple_of(n * chunk, chunk), chunk)
            part = jnp.dot(bottom[...], dense[trace:, cols], preferred_element_type=jnp.float32)
            total[:, cols] = part + source[:, cols].astype(jnp.float32)
            return 0

        trace = bottom.shape[1]
        chunk = trace // 1
        lax.fori_loop(0, total.shape[1] // chunk, columns, 0)


def second_kernel(turn, half, position, dense, total, left, _, out):
    @pl.when(position[0] == turn)
    def _():
        trace = left.shape[1]
        cols = slice(half * trace, (half + 1) * trace)
        part = jnp.dot(left[...], dense[:trace, cols], preferred_element_type=jnp.float32)
        out[...] = (total[:, cols] + part).astype(out.dtype)


def first(turn, position, dense, source, bottom):
    return pl.pallas_call(
        lambda *refs: first_kernel(turn, *refs),
        out_shape=pltpu.VMEM(source.shape, jnp.float32),
        in_specs=[SMEM] + [VMEM] * 3,
        out_specs=VMEM,
        compiler_params=PARAMS,
        name="first",
    )(position, dense, source, bottom)


def second(turn, half, position, dense, total, left, out):
    return pl.pallas_call(
        lambda *refs: second_kernel(turn, half, *refs),
        out_shape=jax.ShapeDtypeStruct(out.shape, out.dtype),
        in_specs=[SMEM] + [VMEM] * 4,
        out_specs=VMEM,
        input_output_aliases={4: 0},
        compiler_params=PARAMS,
        name="right" if half == 0 else "top",
    )(position, dense, total, left, out)


def pairs(nx, ny, turn, period, across):
    found = []
    for i in range(nx):
        for j in range(ny):
            over, up = (i + 1, j) if across else (i, j + 1)
            if (i + j) % period == turn % period and over < nx and up < ny:
                found.append((i * ny + j, over * ny + up))
    return found


def body(blocks, pattern, local_src, owner):
    nbatch, nsource, width = local_src.shape[2:]
    trace = width // 2
    period = 16
    nx, ny = lax.axis_size("gx"), lax.axis_size("gy")
    dense = assemble(pattern[0, 0], blocks[0, 0], width)
    x, y = lax.axis_index("gx"), lax.axis_index("gy")
    source, right, top = sources((x * ny + y).reshape(1), owner, local_src[0, 0])
    position = (x + y).reshape(1)

    for turn in range(1, nx + ny - 1):
        bottom = lax.ppermute(top, ("gx", "gy"), pairs(nx, ny, turn - 1, period, False))
        left = lax.ppermute(right, ("gx", "gy"), pairs(nx, ny, turn - 1, period, True))
        total = first(turn, position, dense, source, bottom)
        top = second(turn, 1, position, dense, total, left, top)
        right = second(turn, 0, position, dense, total, left, right)
    result = jnp.concatenate([right, top], axis=1)
    return result.reshape(1, 1, nbatch, nsource, width)


def solution(mesh):
    return jax.shard_map(
        body,
        mesh=mesh,
        in_specs=(
            P("gx", "gy", None, None, None),
            P("gx", "gy", None),
            P("gx", "gy", None, None, None),
            P(),
        ),
        out_specs=P("gx", "gy", None, None, None),
        check_vma=False,
    )
```

```python
import jax
import jax.numpy as jnp
from jax import lax
from jax.experimental import pallas as pl
from jax.experimental.pallas import tpu as pltpu
from jax.sharding import PartitionSpec as P

VMEM = pl.BlockSpec(memory_space=pltpu.VMEM)
SMEM = pl.BlockSpec(memory_space=pltpu.SMEM)
HBM = pl.BlockSpec(memory_space=pltpu.HBM)
PIECES = 8
PARAMS = pltpu.CompilerParams(vmem_limit_bytes=4 * 2**20)


def assemble_kernel(_, pattern, blocks, dense, pat, blk, pat_done, blk_done):
    count, order, _ = blk.shape
    nblk = dense.shape[0] // order
    pieces = blk_done.shape[0]
    piece = count // pieces
    pat_copy = pltpu.make_async_copy(pattern, pat, pat_done)
    pat_copy.start()

    def blk_copy(p):
        part = pl.ds(p * piece, piece)
        return pltpu.make_async_copy(blocks.at[part], blk.at[part], blk_done.at[p])

    for p in range(pieces):
        blk_copy(p).start()
    dense[...] = jnp.zeros_like(dense)
    pat_copy.wait()

    def settle(p, _):
        blk_copy(p).wait()

        def place(n, _):
            k = p * piece + n
            row = pl.multiple_of(pat[k] // nblk * order, order)
            col = pl.multiple_of(pat[k] % nblk * order, order)
            dense[pl.ds(col, order), pl.ds(row, order)] = blk[k].T
            return 0

        lax.fori_loop(0, piece, place, 0, unroll=8)
        return 0

    lax.fori_loop(0, pieces, settle, 0)


def assemble(part, pat, blk, width):
    return pl.pallas_call(
        assemble_kernel,
        out_shape=pltpu.VMEM((width, width), blk.dtype),
        in_specs=[SMEM, HBM, HBM],
        out_specs=VMEM,
        scratch_shapes=[
            pltpu.SMEM(pat.shape, pat.dtype),
            pltpu.VMEM(blk.shape, blk.dtype),
            pltpu.SemaphoreType.DMA,
            pltpu.SemaphoreType.DMA((PIECES,)),
        ],
        compiler_params=pltpu.CompilerParams(vmem_limit_bytes=8 * 2**20),
        name="assemble",
    )(part, pltpu.with_memory_space_constraint(pat, pltpu.HBM), pltpu.with_memory_space_constraint(blk, pltpu.HBM))


def source_kernel(cell, owner, local, source, right, top, held, who, local_done, who_done):
    local_copy = pltpu.make_async_copy(local, held, local_done)
    who_copy = pltpu.make_async_copy(owner, who, who_done)
    who_copy.start()
    local_copy.start()
    nbatch, nsource, width = held.shape
    trace = width // 2
    square = (nsource, nsource)
    diagonal = lax.broadcasted_iota(jnp.int32, square, 0) == lax.broadcasted_iota(jnp.int32, square, 1)
    who_copy.wait()
    mine = []
    for b in range(nbatch):
        row = jnp.broadcast_to((who[b : b + 1, :] == cell[0]).astype(jnp.float32), square)
        mine.append(jnp.max(jnp.where(diagonal, row, 0.0), axis=1, keepdims=True) > 0.0)
    local_copy.wait()
    for b in range(nbatch):
        rows = slice(b * nsource, (b + 1) * nsource)
        own = jnp.where(mine[b], held[b].astype(jnp.float32), 0.0).astype(source.dtype)
        source[rows, :] = own
        right[rows, :] = own[:, :trace]
        top[rows, :] = own[:, trace:]


def sources(cell, owner, local):
    nbatch, nsource, width = local.shape
    rows = nbatch * nsource
    half = jax.ShapeDtypeStruct((rows, width // 2), local.dtype)
    return pl.pallas_call(
        source_kernel,
        out_shape=(jax.ShapeDtypeStruct((rows, width), local.dtype), half, half),
        in_specs=[SMEM, HBM, HBM],
        out_specs=(VMEM, VMEM, VMEM),
        scratch_shapes=[
            pltpu.VMEM(local.shape, local.dtype),
            pltpu.VMEM(owner.shape, owner.dtype),
            pltpu.SemaphoreType.DMA,
            pltpu.SemaphoreType.DMA,
        ],
        compiler_params=PARAMS,
        name="sources",
    )(cell, pltpu.with_memory_space_constraint(owner, pltpu.HBM), pltpu.with_memory_space_constraint(local, pltpu.HBM))


def touch_kernel(dense, after, out):
    out[...] = dense[: out.shape[0], : out.shape[1]]


def touch(dense, after):
    return pl.pallas_call(
        touch_kernel,
        out_shape=jax.ShapeDtypeStruct((16, 128), dense.dtype),
        in_specs=[VMEM, pl.BlockSpec(memory_space=pl.ANY)],
        out_specs=VMEM,
        compiler_params=PARAMS,
        name="touch",
    )(dense, after)


def first_kernel(turn, position, dense, source, bottom, *refs):
    total = refs[-1]

    @pl.when(position[0] == turn)
    def _():
        trace = bottom.shape[1]
        part = jnp.dot(bottom[...], dense[trace:], preferred_element_type=jnp.float32)
        total[...] = part + source[...].astype(jnp.float32)


def second_kernel(turn, half, position, dense, total, left, swapped, _, out):
    @pl.when(position[0] == turn)
    def _():
        trace = left.shape[1]
        cols = slice(half * trace, (half + 1) * trace)
        given = jnp.where(position[1] == 1, swapped[...], left[...])
        part = jnp.dot(given, dense[:trace, cols], preferred_element_type=jnp.float32)
        out[...] = (total[:, cols] + part).astype(out.dtype)


def first(turn, position, dense, source, bottom, *after):
    return pl.pallas_call(
        lambda *refs: first_kernel(turn, *refs),
        out_shape=pltpu.VMEM(source.shape, jnp.float32),
        in_specs=[SMEM] + [VMEM] * 3 + [pl.BlockSpec(memory_space=pl.ANY)] * len(after),
        out_specs=VMEM,
        compiler_params=PARAMS,
        name="first",
    )(position, dense, source, bottom, *after)


def second(turn, half, position, dense, total, left, swapped, out):
    return pl.pallas_call(
        lambda *refs: second_kernel(turn, half, *refs),
        out_shape=jax.ShapeDtypeStruct(out.shape, out.dtype),
        in_specs=[SMEM] + [VMEM] * 5,
        out_specs=VMEM,
        input_output_aliases={5: 0},
        compiler_params=PARAMS,
        name="right" if half == 0 else "top",
    )(position, dense, total, left, swapped, out)


def pairs(nx, ny, turn, period, across):
    found = []
    for i in range(nx):
        for j in range(ny):
            over, up = (i + 1, j) if across else (i, j + 1)
            if (i + j) % period == turn % period and over < nx and up < ny and not (across and over % 2):
                found.append((i * ny + j, over * ny + up))
    return found


def body(blocks, pattern, local_src, owner):
    nbatch, nsource, width = local_src.shape[2:]
    trace = width // 2
    period = 15
    nx, ny = lax.axis_size("gx"), lax.axis_size("gy")
    x, y = lax.axis_index("gx"), lax.axis_index("gy")
    source, right, top = sources((x * ny + y).reshape(1), owner, local_src[0, 0])
    position = jnp.stack([x + y, x & 1])
    mates = [(cell, cell ^ ny) for cell in range(nx * ny)]

    def sweep(part, outs):
        right, top = outs
        ahead = position - jnp.stack([part * period, 0])
        dense = assemble(ahead, pattern[0, 0], blocks[0, 0], width)
        for turn in range(1, period + 1):
            bottom = lax.ppermute(top, ("gx", "gy"), pairs(nx, ny, turn - 1, period, False))
            swapped = lax.ppermute(right, ("gx", "gy"), mates)
            left = lax.ppermute(right, ("gx", "gy"), pairs(nx, ny, turn - 1, period, True))
            after = [touch(dense, right)] if turn == period else []
            total = first(turn, ahead, dense, source, bottom, *after)
            top = second(turn, 1, ahead, dense, total, left, swapped, top)
            right = second(turn, 0, ahead, dense, total, left, swapped, right)
        return right, top

    right, top = lax.fori_loop(0, (nx + ny - 2) // period, sweep, (right, top))
    result = jnp.concatenate([right, top], axis=1)
    return result.reshape(1, 1, nbatch, nsource, width)


def solution(mesh):
    return jax.shard_map(
        body,
        mesh=mesh,
        in_specs=(
            P("gx", "gy", None, None, None),
            P("gx", "gy", None),
            P("gx", "gy", None, None, None),
            P(),
        ),
        out_specs=P("gx", "gy", None, None, None),
        check_vma=False,
    )
```

```python
import jax
import jax.numpy as jnp
from jax import lax
from jax.experimental import pallas as pl
from jax.experimental.pallas import tpu as pltpu
from jax.sharding import PartitionSpec as P

VMEM = pl.BlockSpec(memory_space=pltpu.VMEM)
SMEM = pl.BlockSpec(memory_space=pltpu.SMEM)
HBM = pl.BlockSpec(memory_space=pltpu.HBM)
PIECES = 8
PARAMS = pltpu.CompilerParams(vmem_limit_bytes=4 * 2**20)


def assemble_kernel(_, pattern, blocks, dense, pat, blk, pat_done, blk_done):
    count, order, _ = blk.shape
    nblk = dense.shape[0] // order
    pieces = blk_done.shape[0]
    piece = count // pieces
    pat_copy = pltpu.make_async_copy(pattern, pat, pat_done)
    pat_copy.start()

    def blk_copy(p):
        part = pl.ds(p * piece, piece)
        return pltpu.make_async_copy(blocks.at[part], blk.at[part], blk_done.at[p])

    for p in range(pieces):
        blk_copy(p).start()
    dense[...] = jnp.zeros_like(dense)
    pat_copy.wait()

    def settle(p, _):
        blk_copy(p).wait()

        def place(n, _):
            k = p * piece + n
            row = pl.multiple_of(pat[k] // nblk * order, order)
            col = pl.multiple_of(pat[k] % nblk * order, order)
            dense[pl.ds(col, order), pl.ds(row, order)] = blk[k].T
            return 0

        lax.fori_loop(0, piece, place, 0, unroll=8)
        return 0

    lax.fori_loop(0, pieces, settle, 0)


def assemble(part, pat, blk, width):
    return pl.pallas_call(
        assemble_kernel,
        out_shape=pltpu.VMEM((width, width), blk.dtype),
        in_specs=[SMEM, HBM, HBM],
        out_specs=VMEM,
        scratch_shapes=[
            pltpu.SMEM(pat.shape, pat.dtype),
            pltpu.VMEM(blk.shape, blk.dtype),
            pltpu.SemaphoreType.DMA,
            pltpu.SemaphoreType.DMA((PIECES,)),
        ],
        compiler_params=pltpu.CompilerParams(vmem_limit_bytes=8 * 2**20),
        name="assemble",
    )(part, pltpu.with_memory_space_constraint(pat, pltpu.HBM), pltpu.with_memory_space_constraint(blk, pltpu.HBM))


def source_kernel(cell, owner, local, source, right, top, held, who, local_done, who_done):
    local_copy = pltpu.make_async_copy(local, held, local_done)
    who_copy = pltpu.make_async_copy(owner, who, who_done)
    who_copy.start()
    local_copy.start()
    nbatch, nsource, width = held.shape
    trace = width // 2
    square = (nsource, nsource)
    diagonal = lax.broadcasted_iota(jnp.int32, square, 0) == lax.broadcasted_iota(jnp.int32, square, 1)
    who_copy.wait()
    mine = []
    for b in range(nbatch):
        row = jnp.broadcast_to((who[b : b + 1, :] == cell[0]).astype(jnp.float32), square)
        mine.append(jnp.max(jnp.where(diagonal, row, 0.0), axis=1, keepdims=True) > 0.0)
    local_copy.wait()
    for b in range(nbatch):
        rows = slice(b * nsource, (b + 1) * nsource)
        own = jnp.where(mine[b], held[b].astype(jnp.float32), 0.0).astype(source.dtype)
        source[rows, :] = own
        right[rows, :] = own[:, :trace]
        top[rows, :] = own[:, trace:]


def sources(cell, owner, local):
    nbatch, nsource, width = local.shape
    rows = nbatch * nsource
    half = jax.ShapeDtypeStruct((rows, width // 2), local.dtype)
    return pl.pallas_call(
        source_kernel,
        out_shape=(jax.ShapeDtypeStruct((rows, width), local.dtype), half, half),
        in_specs=[SMEM, HBM, HBM],
        out_specs=(VMEM, VMEM, VMEM),
        scratch_shapes=[
            pltpu.VMEM(local.shape, local.dtype),
            pltpu.VMEM(owner.shape, owner.dtype),
            pltpu.SemaphoreType.DMA,
            pltpu.SemaphoreType.DMA,
        ],
        compiler_params=PARAMS,
        name="sources",
    )(cell, pltpu.with_memory_space_constraint(owner, pltpu.HBM), pltpu.with_memory_space_constraint(local, pltpu.HBM))


def touch_kernel(dense, after, out):
    out[...] = dense[: out.shape[0], : out.shape[1]]


def touch(dense, after):
    return pl.pallas_call(
        touch_kernel,
        out_shape=jax.ShapeDtypeStruct((16, 128), dense.dtype),
        in_specs=[VMEM, pl.BlockSpec(memory_space=pl.ANY)],
        out_specs=VMEM,
        compiler_params=PARAMS,
        name="touch",
    )(dense, after)


def first_kernel(turn, position, dense, source, bottom, *refs):
    total = refs[-1]

    @pl.when(position[0] == turn)
    def _():
        trace = bottom.shape[1]
        part = jnp.dot(bottom[...], dense[trace:], preferred_element_type=jnp.float32)
        total[...] = part + source[...].astype(jnp.float32)


def second_kernel(turn, half, position, dense, total, left, _, out):
    @pl.when(position[0] == turn)
    def _():
        trace = left.shape[1]
        cols = slice(half * trace, (half + 1) * trace)
        part = jnp.dot(left[...], dense[:trace, cols], preferred_element_type=jnp.float32)
        out[...] = (total[:, cols] + part).astype(out.dtype)


def first(turn, position, dense, source, bottom, *after):
    return pl.pallas_call(
        lambda *refs: first_kernel(turn, *refs),
        out_shape=pltpu.VMEM(source.shape, jnp.float32),
        in_specs=[SMEM] + [VMEM] * 3 + [pl.BlockSpec(memory_space=pl.ANY)] * len(after),
        out_specs=VMEM,
        compiler_params=PARAMS,
        name="first",
    )(position, dense, source, bottom, *after)


def second(turn, half, position, dense, total, left, out):
    return pl.pallas_call(
        lambda *refs: second_kernel(turn, half, *refs),
        out_shape=jax.ShapeDtypeStruct(out.shape, out.dtype),
        in_specs=[SMEM] + [VMEM] * 4,
        out_specs=VMEM,
        input_output_aliases={4: 0},
        compiler_params=PARAMS,
        name="right" if half == 0 else "top",
    )(position, dense, total, left, out)


def pairs(nx, ny, turn, period, across):
    found = []
    for i in range(nx):
        for j in range(ny):
            over, up = (i + 1, j) if across else (i, j + 1)
            if (i + j) % period == turn % period and over < nx and up < ny:
                found.append((i * ny + j, over * ny + up))
    return found


def body(blocks, pattern, local_src, owner):
    nbatch, nsource, width = local_src.shape[2:]
    trace = width // 2
    period = 15
    nx, ny = lax.axis_size("gx"), lax.axis_size("gy")
    x, y = lax.axis_index("gx"), lax.axis_index("gy")
    source, right, top = sources((x * ny + y).reshape(1), owner, local_src[0, 0])
    position = (x + y).reshape(1)

    def sweep(part, outs):
        right, top = outs
        ahead = position - part * period
        dense = assemble(ahead, pattern[0, 0], blocks[0, 0], width)
        for turn in range(1, period + 1):
            bottom = lax.ppermute(top, ("gx", "gy"), pairs(nx, ny, turn - 1, period, False))
            left = lax.ppermute(right, ("gx", "gy"), pairs(nx, ny, turn - 1, period, True))
            after = [touch(dense, right)] if turn == period else []
            total = first(turn, ahead, dense, source, bottom, *after)
            top = second(turn, 1, ahead, dense, total, left, top)
            right = second(turn, 0, ahead, dense, total, left, right)
        return right, top

    right, top = lax.fori_loop(0, (nx + ny - 2) // period, sweep, (right, top))
    result = jnp.concatenate([right, top], axis=1)
    return result.reshape(1, 1, nbatch, nsource, width)


def solution(mesh):
    return jax.shard_map(
        body,
        mesh=mesh,
        in_specs=(
            P("gx", "gy", None, None, None),
            P("gx", "gy", None),
            P("gx", "gy", None, None, None),
            P(),
        ),
        out_specs=P("gx", "gy", None, None, None),
        check_vma=False,
    )
```

```python
import jax
import jax.numpy as jnp
from jax import lax
from jax.experimental import pallas as pl
from jax.experimental.pallas import tpu as pltpu
from jax.sharding import PartitionSpec as P

VMEM = pl.BlockSpec(memory_space=pltpu.VMEM)
SMEM = pl.BlockSpec(memory_space=pltpu.SMEM)
HBM = pl.BlockSpec(memory_space=pltpu.HBM)
PIECES = 8
PARAMS = pltpu.CompilerParams(vmem_limit_bytes=4 * 2**20)


def assemble_kernel(_, pattern, blocks, dense, pat, blk, pat_done, blk_done):
    count, order, _ = blk.shape
    nblk = dense.shape[0] // order
    pieces = blk_done.shape[0]
    piece = count // pieces
    pat_copy = pltpu.make_async_copy(pattern, pat, pat_done)
    pat_copy.start()

    def blk_copy(p):
        part = pl.ds(p * piece, piece)
        return pltpu.make_async_copy(blocks.at[part], blk.at[part], blk_done.at[p])

    for p in range(pieces):
        blk_copy(p).start()
    dense[...] = jnp.zeros_like(dense)
    pat_copy.wait()

    def settle(p, _):
        blk_copy(p).wait()

        def place(n, _):
            k = p * piece + n
            row = pl.multiple_of(pat[k] // nblk * order, order)
            col = pl.multiple_of(pat[k] % nblk * order, order)
            dense[pl.ds(col, order), pl.ds(row, order)] = blk[k].T
            return 0

        lax.fori_loop(0, piece, place, 0, unroll=8)
        return 0

    lax.fori_loop(0, pieces, settle, 0)


def assemble(part, pat, blk, width):
    return pl.pallas_call(
        assemble_kernel,
        out_shape=pltpu.VMEM((width, width), blk.dtype),
        in_specs=[SMEM, HBM, HBM],
        out_specs=VMEM,
        scratch_shapes=[
            pltpu.SMEM(pat.shape, pat.dtype),
            pltpu.VMEM(blk.shape, blk.dtype),
            pltpu.SemaphoreType.DMA,
            pltpu.SemaphoreType.DMA((PIECES,)),
        ],
        compiler_params=pltpu.CompilerParams(vmem_limit_bytes=8 * 2**20),
        name="assemble",
    )(part, pltpu.with_memory_space_constraint(pat, pltpu.HBM), pltpu.with_memory_space_constraint(blk, pltpu.HBM))


def source_kernel(cell, owner, local, source, right, top, held, who, local_done, who_done):
    local_copy = pltpu.make_async_copy(local, held, local_done)
    who_copy = pltpu.make_async_copy(owner, who, who_done)
    who_copy.start()
    local_copy.start()
    nbatch, nsource, width = held.shape
    trace = width // 2
    square = (nsource, nsource)
    diagonal = lax.broadcasted_iota(jnp.int32, square, 0) == lax.broadcasted_iota(jnp.int32, square, 1)
    who_copy.wait()
    mine = []
    for b in range(nbatch):
        row = jnp.broadcast_to((who[b : b + 1, :] == cell[0]).astype(jnp.float32), square)
        mine.append(jnp.max(jnp.where(diagonal, row, 0.0), axis=1, keepdims=True) > 0.0)
    local_copy.wait()
    for b in range(nbatch):
        rows = slice(b * nsource, (b + 1) * nsource)
        own = jnp.where(mine[b], held[b].astype(jnp.float32), 0.0).astype(source.dtype)
        source[rows, :] = own
        right[rows, :] = own[:, :trace]
        top[rows, :] = own[:, trace:]


def sources(cell, owner, local):
    nbatch, nsource, width = local.shape
    rows = nbatch * nsource
    half = jax.ShapeDtypeStruct((rows, width // 2), local.dtype)
    return pl.pallas_call(
        source_kernel,
        out_shape=(jax.ShapeDtypeStruct((rows, width), local.dtype), half, half),
        in_specs=[SMEM, HBM, HBM],
        out_specs=(VMEM, VMEM, VMEM),
        scratch_shapes=[
            pltpu.VMEM(local.shape, local.dtype),
            pltpu.VMEM(owner.shape, owner.dtype),
            pltpu.SemaphoreType.DMA,
            pltpu.SemaphoreType.DMA,
        ],
        compiler_params=PARAMS,
        name="sources",
    )(cell, pltpu.with_memory_space_constraint(owner, pltpu.HBM), pltpu.with_memory_space_constraint(local, pltpu.HBM))


def touch_kernel(dense, after, out):
    out[...] = dense[: out.shape[0], : out.shape[1]]


def touch(dense, after):
    return pl.pallas_call(
        touch_kernel,
        out_shape=jax.ShapeDtypeStruct((16, 128), dense.dtype),
        in_specs=[VMEM, pl.BlockSpec(memory_space=pl.ANY)],
        out_specs=VMEM,
        compiler_params=PARAMS,
        name="touch",
    )(dense, after)


def first_kernel(turn, position, dense, source, bottom, *refs):
    total = refs[-1]

    @pl.when(position[0] == turn)
    def _():
        trace = bottom.shape[1]
        part = jnp.dot(bottom[...], dense[trace:], preferred_element_type=jnp.float32)
        total[...] = part + source[...].astype(jnp.float32)


def second_kernel(turn, half, position, dense, total, left, _, out):
    @pl.when(position[0] == turn)
    def _():
        trace = left.shape[1]
        cols = slice(half * trace, (half + 1) * trace)
        part = jnp.dot(left[...], dense[:trace, cols], preferred_element_type=jnp.float32)
        out[...] = (total[:, cols] + part).astype(out.dtype)


def first(turn, position, dense, source, bottom, *after):
    return pl.pallas_call(
        lambda *refs: first_kernel(turn, *refs),
        out_shape=pltpu.VMEM(source.shape, jnp.float32),
        in_specs=[SMEM] + [VMEM] * 3 + [pl.BlockSpec(memory_space=pl.ANY)] * len(after),
        out_specs=VMEM,
        compiler_params=PARAMS,
        name="first",
    )(position, dense, source, bottom, *after)


def second(turn, half, position, dense, total, left, out):
    return pl.pallas_call(
        lambda *refs: second_kernel(turn, half, *refs),
        out_shape=jax.ShapeDtypeStruct(out.shape, out.dtype),
        in_specs=[SMEM] + [VMEM] * 4,
        out_specs=VMEM,
        input_output_aliases={4: 0},
        compiler_params=PARAMS,
        name="right" if half == 0 else "top",
    )(position, dense, total, left, out)


def pairs(nx, ny, turn, period, across):
    found = []
    for i in range(nx):
        for j in range(ny):
            over, up = (i + 1, j) if across else (i, j + 1)
            if (i + j) % period == turn % period and over < nx and up < ny:
                found.append((i * ny + j, over * ny + up))
    return found


def body(blocks, pattern, local_src, owner):
    nbatch, nsource, width = local_src.shape[2:]
    trace = width // 2
    period = 14
    nx, ny = lax.axis_size("gx"), lax.axis_size("gy")
    x, y = lax.axis_index("gx"), lax.axis_index("gy")
    source, right, top = sources((x * ny + y).reshape(1), owner, local_src[0, 0])
    position = (x + y).reshape(1)

    def sweep(part, outs, turns, again):
        right, top = outs
        ahead = position - part * period
        dense = assemble(ahead, pattern[0, 0], blocks[0, 0], width)
        for turn in range(1, turns + 1):
            bottom = lax.ppermute(top, ("gx", "gy"), pairs(nx, ny, turn - 1, period, False))
            left = lax.ppermute(right, ("gx", "gy"), pairs(nx, ny, turn - 1, period, True))
            after = [touch(dense, right)] if again and turn == turns else []
            total = first(turn, ahead, dense, source, bottom, *after)
            top = second(turn, 1, ahead, dense, total, left, top)
            right = second(turn, 0, ahead, dense, total, left, right)
        return right, top

    parts, rest = divmod(nx + ny - 2, period)
    outs = lax.fori_loop(0, parts, lambda part, outs: sweep(part, outs, period, True), (right, top))
    right, top = sweep(parts, outs, rest, False)
    result = jnp.concatenate([right, top], axis=1)
    return result.reshape(1, 1, nbatch, nsource, width)


def solution(mesh):
    return jax.shard_map(
        body,
        mesh=mesh,
        in_specs=(
            P("gx", "gy", None, None, None),
            P("gx", "gy", None),
            P("gx", "gy", None, None, None),
            P(),
        ),
        out_specs=P("gx", "gy", None, None, None),
        check_vma=False,
    )
```

```python
import jax
import jax.numpy as jnp
from jax import lax
from jax.experimental import pallas as pl
from jax.experimental.pallas import tpu as pltpu
from jax.sharding import PartitionSpec as P

VMEM = pl.BlockSpec(memory_space=pltpu.VMEM)
SMEM = pl.BlockSpec(memory_space=pltpu.SMEM)
HBM = pl.BlockSpec(memory_space=pltpu.HBM)
PIECES = 8
PARAMS = pltpu.CompilerParams(vmem_limit_bytes=4 * 2**20)


def assemble_kernel(_, pattern, blocks, dense, pat, blk, pat_done, blk_done):
    count, order, _ = blk.shape
    nblk = dense.shape[0] // order
    pieces = blk_done.shape[0]
    piece = count // pieces
    pat_copy = pltpu.make_async_copy(pattern, pat, pat_done)
    pat_copy.start()

    def blk_copy(p):
        part = pl.ds(p * piece, piece)
        return pltpu.make_async_copy(blocks.at[part], blk.at[part], blk_done.at[p])

    for p in range(pieces):
        blk_copy(p).start()
    dense[...] = jnp.zeros_like(dense)
    pat_copy.wait()

    def settle(p, _):
        blk_copy(p).wait()

        def place(n, _):
            k = p * piece + n
            row = pl.multiple_of(pat[k] // nblk * order, order)
            col = pl.multiple_of(pat[k] % nblk * order, order)
            dense[pl.ds(col, order), pl.ds(row, order)] = blk[k].T
            return 0

        lax.fori_loop(0, piece, place, 0, unroll=8)
        return 0

    lax.fori_loop(0, pieces, settle, 0)


def assemble(part, pat, blk, width):
    return pl.pallas_call(
        assemble_kernel,
        out_shape=pltpu.VMEM((width, width), blk.dtype),
        in_specs=[SMEM, HBM, HBM],
        out_specs=VMEM,
        scratch_shapes=[
            pltpu.SMEM(pat.shape, pat.dtype),
            pltpu.VMEM(blk.shape, blk.dtype),
            pltpu.SemaphoreType.DMA,
            pltpu.SemaphoreType.DMA((PIECES,)),
        ],
        compiler_params=pltpu.CompilerParams(vmem_limit_bytes=8 * 2**20),
        name="assemble",
    )(part, pltpu.with_memory_space_constraint(pat, pltpu.HBM), pltpu.with_memory_space_constraint(blk, pltpu.HBM))


def source_kernel(cell, owner, local, source, right, top, held, who, local_done, who_done):
    local_copy = pltpu.make_async_copy(local, held, local_done)
    who_copy = pltpu.make_async_copy(owner, who, who_done)
    who_copy.start()
    local_copy.start()
    nbatch, nsource, width = held.shape
    trace = width // 2
    square = (nsource, nsource)
    diagonal = lax.broadcasted_iota(jnp.int32, square, 0) == lax.broadcasted_iota(jnp.int32, square, 1)
    who_copy.wait()
    mine = []
    for b in range(nbatch):
        row = jnp.broadcast_to((who[b : b + 1, :] == cell[0]).astype(jnp.float32), square)
        mine.append(jnp.max(jnp.where(diagonal, row, 0.0), axis=1, keepdims=True) > 0.0)
    local_copy.wait()
    for b in range(nbatch):
        rows = slice(b * nsource, (b + 1) * nsource)
        own = jnp.where(mine[b], held[b].astype(jnp.float32), 0.0).astype(source.dtype)
        source[rows, :] = own
        right[rows, :] = own[:, :trace]
        top[rows, :] = own[:, trace:]


def sources(cell, owner, local):
    nbatch, nsource, width = local.shape
    rows = nbatch * nsource
    half = jax.ShapeDtypeStruct((rows, width // 2), local.dtype)
    return pl.pallas_call(
        source_kernel,
        out_shape=(jax.ShapeDtypeStruct((rows, width), local.dtype), half, half),
        in_specs=[SMEM, HBM, HBM],
        out_specs=(VMEM, VMEM, VMEM),
        scratch_shapes=[
            pltpu.VMEM(local.shape, local.dtype),
            pltpu.VMEM(owner.shape, owner.dtype),
            pltpu.SemaphoreType.DMA,
            pltpu.SemaphoreType.DMA,
        ],
        compiler_params=PARAMS,
        name="sources",
    )(cell, pltpu.with_memory_space_constraint(owner, pltpu.HBM), pltpu.with_memory_space_constraint(local, pltpu.HBM))


def touch_kernel(dense, after, out):
    out[...] = dense[: out.shape[0], : out.shape[1]]


def touch(dense, after):
    return pl.pallas_call(
        touch_kernel,
        out_shape=jax.ShapeDtypeStruct((16, 128), dense.dtype),
        in_specs=[VMEM, pl.BlockSpec(memory_space=pl.ANY)],
        out_specs=VMEM,
        compiler_params=PARAMS,
        name="touch",
    )(dense, after)


def first_kernel(turn, position, dense, source, left, *refs):
    total = refs[-1]

    @pl.when(position[0] == turn)
    def _():
        trace = left.shape[1]
        part = jnp.dot(left[...], dense[:trace], preferred_element_type=jnp.float32)
        total[...] = part + source[...].astype(jnp.float32)


def second_kernel(turn, half, position, dense, total, bottom, _, out):
    @pl.when(position[0] == turn)
    def _():
        trace = bottom.shape[1]
        cols = slice(half * trace, (half + 1) * trace)
        part = jnp.dot(bottom[...], dense[trace:, cols], preferred_element_type=jnp.float32)
        out[...] = (total[:, cols] + part).astype(out.dtype)


def first(turn, position, dense, source, left, *after):
    return pl.pallas_call(
        lambda *refs: first_kernel(turn, *refs),
        out_shape=pltpu.VMEM(source.shape, jnp.float32),
        in_specs=[SMEM] + [VMEM] * 3 + [pl.BlockSpec(memory_space=pl.ANY)] * len(after),
        out_specs=VMEM,
        compiler_params=PARAMS,
        name="first",
    )(position, dense, source, left, *after)


def second(turn, half, position, dense, total, bottom, out):
    return pl.pallas_call(
        lambda *refs: second_kernel(turn, half, *refs),
        out_shape=jax.ShapeDtypeStruct(out.shape, out.dtype),
        in_specs=[SMEM] + [VMEM] * 4,
        out_specs=VMEM,
        input_output_aliases={4: 0},
        compiler_params=PARAMS,
        name="right" if half == 0 else "top",
    )(position, dense, total, bottom, out)


def pairs(nx, ny, turn, period, across):
    found = []
    for i in range(nx):
        for j in range(ny):
            over, up = (i + 1, j) if across else (i, j + 1)
            if (i + j) % period == turn % period and over < nx and up < ny:
                found.append((i * ny + j, over * ny + up))
    return found


def body(blocks, pattern, local_src, owner):
    nbatch, nsource, width = local_src.shape[2:]
    trace = width // 2
    period = 14
    nx, ny = lax.axis_size("gx"), lax.axis_size("gy")
    x, y = lax.axis_index("gx"), lax.axis_index("gy")
    source, right, top = sources((x * ny + y).reshape(1), owner, local_src[0, 0])
    position = (x + y).reshape(1)

    def sweep(part, outs, turns, again):
        right, top = outs
        ahead = position - part * period
        dense = assemble(ahead, pattern[0, 0], blocks[0, 0], width)
        for turn in range(1, turns + 1):
            left = lax.ppermute(right, ("gx", "gy"), pairs(nx, ny, turn - 1, period, True))
            bottom = lax.ppermute(top, ("gx", "gy"), pairs(nx, ny, turn - 1, period, False))
            after = [touch(dense, top)] if again and turn == turns else []
            total = first(turn, ahead, dense, source, left, *after)
            right = second(turn, 0, ahead, dense, total, bottom, right)
            top = second(turn, 1, ahead, dense, total, bottom, top)
        return right, top

    parts, rest = divmod(nx + ny - 2, period)
    outs = lax.fori_loop(0, parts, lambda part, outs: sweep(part, outs, period, True), (right, top))
    right, top = sweep(parts, outs, rest, False)
    result = jnp.concatenate([right, top], axis=1)
    return result.reshape(1, 1, nbatch, nsource, width)


def solution(mesh):
    return jax.shard_map(
        body,
        mesh=mesh,
        in_specs=(
            P("gx", "gy", None, None, None),
            P("gx", "gy", None),
            P("gx", "gy", None, None, None),
            P(),
        ),
        out_specs=P("gx", "gy", None, None, None),
        check_vma=False,
    )
```

```python
import jax
import jax.numpy as jnp
from jax import lax
from jax.experimental import pallas as pl
from jax.experimental.pallas import tpu as pltpu
from jax.sharding import PartitionSpec as P

VMEM = pl.BlockSpec(memory_space=pltpu.VMEM)
SMEM = pl.BlockSpec(memory_space=pltpu.SMEM)
HBM = pl.BlockSpec(memory_space=pltpu.HBM)
PIECES = 8
PARAMS = pltpu.CompilerParams(vmem_limit_bytes=4 * 2**20)


def assemble_kernel(_, pattern, blocks, dense, pat, blk, pat_done, blk_done):
    count, order, _ = blk.shape
    nblk = dense.shape[0] // order
    pieces = blk_done.shape[0]
    piece = count // pieces
    pat_copy = pltpu.make_async_copy(pattern, pat, pat_done)
    pat_copy.start()

    def blk_copy(p):
        part = pl.ds(p * piece, piece)
        return pltpu.make_async_copy(blocks.at[part], blk.at[part], blk_done.at[p])

    for p in range(pieces):
        blk_copy(p).start()
    dense[...] = jnp.zeros_like(dense)
    pat_copy.wait()

    def settle(p, _):
        blk_copy(p).wait()

        def place(n, _):
            k = p * piece + n
            row = pl.multiple_of(pat[k] // nblk * order, order)
            col = pl.multiple_of(pat[k] % nblk * order, order)
            dense[pl.ds(col, order), pl.ds(row, order)] = blk[k].T
            return 0

        lax.fori_loop(0, piece, place, 0, unroll=8)
        return 0

    lax.fori_loop(0, pieces, settle, 0)


def assemble(part, pat, blk, width):
    return pl.pallas_call(
        assemble_kernel,
        out_shape=pltpu.VMEM((width, width), blk.dtype),
        in_specs=[SMEM, HBM, HBM],
        out_specs=VMEM,
        scratch_shapes=[
            pltpu.SMEM(pat.shape, pat.dtype),
            pltpu.VMEM(blk.shape, blk.dtype),
            pltpu.SemaphoreType.DMA,
            pltpu.SemaphoreType.DMA((PIECES,)),
        ],
        compiler_params=pltpu.CompilerParams(vmem_limit_bytes=8 * 2**20),
        name="assemble",
    )(part, pltpu.with_memory_space_constraint(pat, pltpu.HBM), pltpu.with_memory_space_constraint(blk, pltpu.HBM))


def source_kernel(cell, owner, local, source, right, top, held, who, local_done, who_done):
    local_copy = pltpu.make_async_copy(local, held, local_done)
    who_copy = pltpu.make_async_copy(owner, who, who_done)
    who_copy.start()
    local_copy.start()
    nbatch, nsource, width = held.shape
    trace = width // 2
    square = (nsource, nsource)
    diagonal = lax.broadcasted_iota(jnp.int32, square, 0) == lax.broadcasted_iota(jnp.int32, square, 1)
    who_copy.wait()
    mine = []
    for b in range(nbatch):
        row = jnp.broadcast_to((who[b : b + 1, :] == cell[0]).astype(jnp.float32), square)
        mine.append(jnp.max(jnp.where(diagonal, row, 0.0), axis=1, keepdims=True) > 0.0)
    local_copy.wait()
    for b in range(nbatch):
        rows = slice(b * nsource, (b + 1) * nsource)
        own = jnp.where(mine[b], held[b].astype(jnp.float32), 0.0).astype(source.dtype)
        source[rows, :] = own
        right[rows, :] = own[:, :trace]
        top[rows, :] = own[:, trace:]


def sources(cell, owner, local):
    nbatch, nsource, width = local.shape
    rows = nbatch * nsource
    half = jax.ShapeDtypeStruct((rows, width // 2), local.dtype)
    return pl.pallas_call(
        source_kernel,
        out_shape=(jax.ShapeDtypeStruct((rows, width), local.dtype), half, half),
        in_specs=[SMEM, HBM, HBM],
        out_specs=(VMEM, VMEM, VMEM),
        scratch_shapes=[
            pltpu.VMEM(local.shape, local.dtype),
            pltpu.VMEM(owner.shape, owner.dtype),
            pltpu.SemaphoreType.DMA,
            pltpu.SemaphoreType.DMA,
        ],
        compiler_params=PARAMS,
        name="sources",
    )(cell, pltpu.with_memory_space_constraint(owner, pltpu.HBM), pltpu.with_memory_space_constraint(local, pltpu.HBM))


def touch_kernel(dense, after, out):
    out[...] = dense[: out.shape[0], : out.shape[1]]


def touch(dense, after):
    return pl.pallas_call(
        touch_kernel,
        out_shape=jax.ShapeDtypeStruct((16, 128), dense.dtype),
        in_specs=[VMEM, pl.BlockSpec(memory_space=pl.ANY)],
        out_specs=VMEM,
        compiler_params=PARAMS,
        name="touch",
    )(dense, after)


def first_kernel(turn, position, dense, source, bottom, *refs):
    total = refs[-1]

    @pl.when(position[0] == turn)
    def _():
        trace = bottom.shape[1]
        part = jnp.dot(bottom[...], dense[trace:], preferred_element_type=jnp.float32)
        total[...] = part + source[...].astype(jnp.float32)


def second_kernel(turn, half, position, dense, total, left, _, out):
    @pl.when(position[0] == turn)
    def _():
        trace = left.shape[1]
        cols = slice(half * trace, (half + 1) * trace)
        part = jnp.dot(left[...], dense[:trace, cols], preferred_element_type=jnp.float32)
        out[...] = (total[:, cols] + part).astype(out.dtype)


def first(turn, position, dense, source, bottom, *after):
    return pl.pallas_call(
        lambda *refs: first_kernel(turn, *refs),
        out_shape=pltpu.VMEM(source.shape, jnp.float32),
        in_specs=[SMEM] + [VMEM] * 3 + [pl.BlockSpec(memory_space=pl.ANY)] * len(after),
        out_specs=VMEM,
        compiler_params=PARAMS,
        name="first",
    )(position, dense, source, bottom, *after)


def second(turn, half, position, dense, total, left, out):
    return pl.pallas_call(
        lambda *refs: second_kernel(turn, half, *refs),
        out_shape=jax.ShapeDtypeStruct(out.shape, out.dtype),
        in_specs=[SMEM] + [VMEM] * 4,
        out_specs=VMEM,
        input_output_aliases={4: 0},
        compiler_params=PARAMS,
        name="right" if half == 0 else "top",
    )(position, dense, total, left, out)


def pairs(nx, ny, turn, period, across):
    found = []
    for i in range(nx):
        for j in range(ny):
            over, up = (i + 1, j) if across else (i, j + 1)
            if (i + j) % period == turn % period and over < nx and up < ny:
                found.append((i * ny + j, over * ny + up))
    return found


def body(blocks, pattern, local_src, owner):
    nbatch, nsource, width = local_src.shape[2:]
    trace = width // 2
    period = 12
    nx, ny = lax.axis_size("gx"), lax.axis_size("gy")
    x, y = lax.axis_index("gx"), lax.axis_index("gy")
    source, right, top = sources((x * ny + y).reshape(1), owner, local_src[0, 0])
    position = (x + y).reshape(1)

    def sweep(part, outs, turns, again):
        right, top = outs
        ahead = position - part * period
        dense = assemble(ahead, pattern[0, 0], blocks[0, 0], width)
        for turn in range(1, turns + 1):
            bottom = lax.ppermute(top, ("gx", "gy"), pairs(nx, ny, turn - 1, period, False))
            left = lax.ppermute(right, ("gx", "gy"), pairs(nx, ny, turn - 1, period, True))
            after = [touch(dense, right)] if again and turn == turns else []
            total = first(turn, ahead, dense, source, bottom, *after)
            top = second(turn, 1, ahead, dense, total, left, top)
            right = second(turn, 0, ahead, dense, total, left, right)
        return right, top

    parts, rest = divmod(nx + ny - 2, period)
    outs = lax.fori_loop(0, parts, lambda part, outs: sweep(part, outs, period, True), (right, top))
    right, top = sweep(parts, outs, rest, False)
    result = jnp.concatenate([right, top], axis=1)
    return result.reshape(1, 1, nbatch, nsource, width)


def solution(mesh):
    return jax.shard_map(
        body,
        mesh=mesh,
        in_specs=(
            P("gx", "gy", None, None, None),
            P("gx", "gy", None),
            P("gx", "gy", None, None, None),
            P(),
        ),
        out_specs=P("gx", "gy", None, None, None),
        check_vma=False,
    )
```
